32 devices in a mesh: row: 8 (over z, y), rep: 4 (over x, core).
Axes of the slice: x: 2, y: 2, z: 4, core: 2. Of those that a mesh axis runs over, the one named last changes fastest.
Arguments:
- features: bfloat16 [8192, 128], P(('row', 'rep')), may hold values from -0.0625 to 0.0625
- grad_out: bfloat16 [8192, 256], P(('row', 'rep')), may hold values from -6 to 6
- weight: bfloat16 [128, 256], replicated, may hold values from -0.375 to 0.375
- tile_vals: bfloat16 [8, 4, 8, 40, 128, 128], P('row', 'rep'), may hold values from -0.0625 to 0.0625
- tile_rows: int32 [8, 4, 8, 40], P('row', 'rep'), may hold values from 0 to 1
- tile_cols: int32 [8, 4, 8, 40], P('row', 'rep'), may hold values from 0 to 7
- tile_counts: int32 [8, 4, 8], P('row', 'rep'), may hold values from 10 to 40, as said below
Outputs:
- input_grad: bfloat16 [8192, 128], P(('row', 'rep'))
- weight_grad: float32 [128, 256], replicated
The draws below stay inside these ranges and needn't reach their ends.
Inputs may be any that keep to these rules, and one draw needn't show every extreme that they name: Only the first tile_counts[b, c, s] slots of a device's offset s are live. In every draw one row block has all 40 slots live at every offset on every piece.
All inputs are finite; a program needn't handle non-finite values.
Results may differ from the reference program's by a relative error of at most 0.001.
Values may be sent and summed in bfloat16 or wider, within the bound.
A program may use at most 128 MiB of HBM per device.

```python
import jax
import jax.numpy as jnp
from jax import lax

F = 128
HID = 256
TILE = 128
ROWS_DEV = 256
TILES = 40
STEPS = 8
ROW_BLOCKS = 8
PIECES = 4
NODES = 8192


def draw_tile_counts(key, part):
    first, second = jax.random.split(key)
    grid_shape = (ROW_BLOCKS, PIECES, STEPS)
    base_counts = jax.random.randint(first, grid_shape, TILES // 4, TILES // 2 + 1, dtype=jnp.int32)
    heavy = jax.random.randint(second, (), 0, ROW_BLOCKS, dtype=jnp.int32)
    block_ids = lax.broadcasted_iota(jnp.int32, grid_shape, 0)
    return jnp.where(block_ids == heavy, TILES, base_counts).astype(jnp.int32)


def plant(result, key, least, largest):
    spot = [jax.random.randint(jax.random.fold_in(key, axis), (), 0, length) for axis, length in enumerate(result.shape)]
    main_axis = result.shape.index(max(result.shape))
    beside = spot[:main_axis] + [(spot[main_axis] + 1) % result.shape[main_axis]] + spot[main_axis + 1:]
    return result.at[tuple(spot)].set(least).at[tuple(beside)].set(largest)


def shard_levels(key, extent, cuts, smallest, high):
    loudness = 1.0
    for axis_at, blocks in cuts:
        draws = jax.random.uniform(jax.random.fold_in(jax.random.fold_in(key, 6), axis_at), (blocks,), jnp.float32, smallest / len(cuts), high / len(cuts))
        loudness = loudness * jnp.repeat(jnp.exp(draws), extent[axis_at] // blocks).reshape((-1,) + (1,) * (len(extent) - 1 - axis_at))
    return loudness


def gaussian(stream_key, dims, width, most, cuts=(), kind=jnp.bfloat16):
    drawn = width * jax.random.normal(stream_key, dims, jnp.float32)
    if cuts:
        drawn = drawn * shard_levels(stream_key, dims, cuts, -0.22, 0.18)
    return jnp.clip(drawn, -most, most).astype(kind)


def setup_inputs(seed: int = 0) -> dict:
    arg_keys = jax.random.split(jax.random.key(seed), 8)
    features = gaussian(arg_keys[0], (NODES, F), NODES ** -0.5, 0.0625, ((0, 32),))
    grad_out = gaussian(arg_keys[1], (NODES, HID), 1.0, 6.0, ((0, 32),))
    weight = gaussian(arg_keys[2], (F, HID), HID ** -0.5, 0.375)
    tile_vals = gaussian(arg_keys[3], (ROW_BLOCKS, PIECES, STEPS, TILES, TILE, TILE), (STEPS * TILES * TILE * TILE * 2 // (5 * ROWS_DEV)) ** -0.5, 0.0625, ((0, 8), (1, 4)))
    tile_rows = plant(jax.random.randint(arg_keys[4], (ROW_BLOCKS, PIECES, STEPS, TILES), 0, ROWS_DEV // TILE), jax.random.fold_in(arg_keys[4], 1), 0, (ROWS_DEV // TILE) - 1).astype(jnp.int32)
    tile_cols = plant(jax.random.randint(arg_keys[5], (ROW_BLOCKS, PIECES, STEPS, TILES), 0, PIECES * ROWS_DEV // TILE), jax.random.fold_in(arg_keys[5], 1), 0, (PIECES * ROWS_DEV // TILE) - 1).astype(jnp.int32)
    tile_counts = draw_tile_counts(jax.random.fold_in(arg_keys[7], 71), 0)
    return {"features": features, "grad_out": grad_out, "weight": weight, "tile_vals": tile_vals, "tile_rows": tile_rows, "tile_cols": tile_cols, "tile_counts": tile_counts}


def reference(features, grad_out, weight, tile_vals, tile_rows, tile_cols, tile_counts):
    tile = tile_vals.shape[-1]
    row_tiles = ROWS_DEV // tile
    col_tiles = PIECES * ROWS_DEV // tile
    pieces = grad_out.reshape(ROW_BLOCKS, PIECES, row_tiles, tile, HID)
    slot_ids = jnp.arange(TILES, dtype=jnp.int32)
    piece_ids = jnp.arange(PIECES, dtype=jnp.int32)[:, None]

    def one_block(block_index):
        totals = jnp.zeros((col_tiles, tile, HID), jnp.float32)
        for step in range(STEPS):
            source_block = ((block_index - step) % ROW_BLOCKS).astype(jnp.int32)
            source = lax.dynamic_index_in_dim(pieces, source_block, 0, keepdims=False)
            values = lax.dynamic_index_in_dim(tile_vals, block_index, 0, keepdims=False)[:, step]
            rows_now = lax.dynamic_index_in_dim(tile_rows, block_index, 0, keepdims=False)[:, step]
            cols_now = lax.dynamic_index_in_dim(tile_cols, block_index, 0, keepdims=False)[:, step]
            counts_now = lax.dynamic_index_in_dim(tile_counts, block_index, 0, keepdims=False)[:, step]
            chosen = source[piece_ids, rows_now]
            live_mask = (slot_ids[None, :] < counts_now[:, None]).astype(jnp.float32)
            contrib = jnp.einsum("ckab,ckaf->ckbf", values.astype(jnp.float32), chosen.astype(jnp.float32))
            contrib = contrib * live_mask[:, :, None, None]
            totals = totals.at[cols_now.reshape(-1)].add(contrib.reshape(-1, tile, HID))
        return totals

    adjoint = lax.map(one_block, jnp.arange(ROW_BLOCKS, dtype=jnp.int32))
    adjoint = adjoint.reshape(ROW_BLOCKS * PIECES * ROWS_DEV, HID)
    input_grad = jnp.dot(adjoint, weight.astype(jnp.float32).T, precision=lax.Precision.HIGHEST).astype(jnp.bfloat16)
    weight_grad = jnp.dot(features.astype(jnp.float32).T, adjoint, precision=lax.Precision.HIGHEST)
    return (input_grad, weight_grad)
```

```python
import functools

import jax
import jax.numpy as jnp
from jax import lax
from jax.experimental import pallas as pl
from jax.experimental.pallas import tpu as pltpu
from jax.sharding import PartitionSpec as P

MESH = pl.DeviceIdType.MESH
GROUP = 4


def gather_kernel(n_row, n_rep, offsets, g_ref, f_ref, gall_ref, fall_ref, send_sem, recv_sem, fsend_sem, frecv_sem, local_sem):
    row, rep = lax.axis_index("row"), lax.axis_index("rep")
    barrier = pltpu.get_barrier_semaphore()
    shifts = sorted({k % n_row for k in range(1, offsets)} | {-k % n_row for k in range(1, offsets)})
    for k in shifts:
        pl.semaphore_signal(barrier, inc=1, device_id=(lax.rem(row + k, n_row), rep), device_id_type=MESH)
    for k in range(1, n_rep):
        pl.semaphore_signal(barrier, inc=1, device_id=(row, lax.rem(rep + k, n_rep)), device_id_type=MESH)
    own_g = pltpu.make_async_copy(g_ref, gall_ref.at[0], local_sem.at[0])
    own_f = pltpu.make_async_copy(f_ref, fall_ref.at[rep], local_sem.at[1])
    own_g.start()
    own_f.start()
    pl.semaphore_wait(barrier, len(shifts) + n_rep - 1)
    copies = []
    for k in range(1, offsets):
        copies.append(pltpu.make_async_remote_copy(
            src_ref=g_ref, dst_ref=gall_ref.at[k], send_sem=send_sem.at[k], recv_sem=recv_sem.at[k],
            device_id=(lax.rem(row + k, n_row), rep), device_id_type=MESH))
    for k in range(1, n_rep):
        copies.append(pltpu.make_async_remote_copy(
            src_ref=f_ref, dst_ref=fall_ref.at[rep], send_sem=fsend_sem.at[k], recv_sem=frecv_sem.at[k],
            device_id=(row, lax.rem(rep + k, n_rep)), device_id_type=MESH))
    for copy in copies:
        copy.start()
    own_g.wait()
    own_f.wait()
    for copy in copies:
        copy.wait()


def gather(grad_out, features, n_row, n_rep, offsets):
    return pl.pallas_call(
        functools.partial(gather_kernel, n_row, n_rep, offsets),
        out_shape=(
            jax.ShapeDtypeStruct((offsets,) + grad_out.shape, grad_out.dtype),
            jax.ShapeDtypeStruct((n_rep,) + features.shape, features.dtype),
        ),
        in_specs=[pl.BlockSpec(memory_space=pl.ANY)] * 2,
        out_specs=(pl.BlockSpec(memory_space=pl.ANY),) * 2,
        scratch_shapes=[
            pltpu.SemaphoreType.DMA((offsets,)),
            pltpu.SemaphoreType.DMA((offsets,)),
            pltpu.SemaphoreType.DMA((n_rep,)),
            pltpu.SemaphoreType.DMA((n_rep,)),
            pltpu.SemaphoreType.DMA((2,)),
        ],
        compiler_params=pltpu.CompilerParams(collective_id=0, has_side_effects=True),
        name="gather_sources",
    )(grad_out, features)


def dot_first(left, right):
    return lax.dot_general(left, right, (((0,), (0,)), ((), ())), preferred_element_type=jnp.float32)


def split(value):
    high = value.astype(jnp.bfloat16)
    low = (value - high.astype(jnp.float32)).astype(jnp.bfloat16)
    return high, low


def tiles_kernel(offsets, slots, tile, row_tiles, col_tiles, rows_ref, cols_ref, counts_ref, vals_ref, gall_ref, fall_ref, weight_ref, ig_ref, wg_ref, vals, blocks, totals, vals_sem, g_sem):
    loads = []
    for s in range(offsets):
        loads.append(pltpu.make_async_copy(vals_ref.at[0, 0, s], vals.at[s], vals_sem.at[s]))
    g_load = pltpu.make_async_copy(gall_ref, blocks.at[pl.ds(0, offsets)], g_sem)
    g_load.start()
    for load in loads:
        load.start()
    totals[...] = jnp.zeros_like(totals)
    blocks[offsets] = jnp.zeros(blocks.shape[1:], blocks.dtype)
    g_load.wait()
    for s in range(offsets):
        loads[s].wait()
        count = counts_ref[0, 0, s]

        def one_group(group, carry, s=s, count=count):
            parts = []
            for u in range(GROUP):
                k = group * GROUP + u
                live = k < count
                block = jnp.where(live, s, offsets)
                chosen = blocks[block, pl.ds(pl.multiple_of(rows_ref[0, 0, s, k] * tile, tile), tile), :]
                parts.append((cols_ref[0, 0, s, k], dot_first(vals[s, k], chosen)))
            for col, part in parts:
                totals[col] += part
            return carry

        lax.fori_loop(0, (count + GROUP - 1) // GROUP, one_group, 0)
    weight = weight_ref[...]
    wg_ref[...] = jnp.zeros_like(wg_ref)

    def one_col(col, carry):
        high, low = split(totals[col])
        dims = (((1,), (1,)), ((), ()))
        ig_ref[col] = (
            lax.dot_general(high, weight, dims, preferred_element_type=jnp.float32)
            + lax.dot_general(low, weight, dims, preferred_element_type=jnp.float32))
        feats = fall_ref[col]
        wg_ref[...] += dot_first(feats, high) + dot_first(feats, low)
        return carry

    lax.fori_loop(0, col_tiles, one_col, 0)


def tile_products(tile_rows, tile_cols, tile_counts, tile_vals, gall, fall, weight):
    offsets, slots, tile = tile_vals.shape[2], tile_vals.shape[3], tile_vals.shape[4]
    rows_dev, hidden = gall.shape[1:]
    n_rep, _, feats = fall.shape
    row_tiles = rows_dev // tile
    col_tiles = n_rep * row_tiles
    smem = pl.BlockSpec(memory_space=pltpu.SMEM)
    vmem = pl.BlockSpec(memory_space=pltpu.VMEM)
    hbm = pl.BlockSpec(memory_space=pl.ANY)
    return pl.pallas_call(
        functools.partial(tiles_kernel, offsets, slots, tile, row_tiles, col_tiles),
        out_shape=(
            jax.ShapeDtypeStruct((col_tiles, tile, feats), jnp.float32),
            jax.ShapeDtypeStruct((feats, hidden), jnp.float32),
        ),
        in_specs=[smem, smem, smem, hbm, hbm, vmem, vmem],
        out_specs=(vmem, vmem),
        scratch_shapes=[
            pltpu.VMEM((offsets, slots, tile, tile), jnp.bfloat16),
            pltpu.VMEM((offsets + 1, rows_dev, hidden), jnp.bfloat16),
            pltpu.VMEM((col_tiles, tile, hidden), jnp.float32),
            pltpu.SemaphoreType.DMA((offsets,)),
            pltpu.SemaphoreType.DMA,
        ],
        compiler_params=pltpu.CompilerParams(vmem_limit_bytes=40 * 2**20),
        name="tile_products",
    )(tile_rows, tile_cols, tile_counts, tile_vals, gall, fall.reshape(col_tiles, tile, feats), weight)


def reduce_kernel(n_row, n_rep, ig_ref, wg_ref, out_ref, wout_ref, ig_buf, wg_buf, row_buf, full_buf, ig_send, ig_recv, wg_send, wg_recv, row_send, row_recv, full_send, full_recv):
    row, rep = lax.axis_index("row"), lax.axis_index("rep")
    part = wg_buf.shape[1]
    barrier = pltpu.get_barrier_semaphore()
    for k in range(1, n_row):
        pl.semaphore_signal(barrier, inc=1, device_id=(lax.rem(row + k, n_row), rep), device_id_type=MESH)
    for k in range(1, n_rep):
        pl.semaphore_signal(barrier, inc=1, device_id=(row, lax.rem(rep + k, n_rep)), device_id_type=MESH)
    pl.semaphore_wait(barrier, n_row + n_rep - 2)

    wg_copies, ig_copies, row_copies, full_copies = [], [], [], []
    for k in range(1, n_rep):
        other = lax.rem(rep + k, n_rep)
        wg_copies.append(pltpu.make_async_remote_copy(
            src_ref=wg_ref.at[other], dst_ref=wg_buf.at[rep], send_sem=wg_send.at[k], recv_sem=wg_recv.at[k],
            device_id=(row, other), device_id_type=MESH))
        ig_copies.append(pltpu.make_async_remote_copy(
            src_ref=ig_ref.at[other], dst_ref=ig_buf.at[rep], send_sem=ig_send.at[k], recv_sem=ig_recv.at[k],
            device_id=(row, other), device_id_type=MESH))
    for copy in wg_copies + ig_copies:
        copy.start()
    wg_buf[rep] = wg_ref[rep]
    ig_buf[rep] = ig_ref[rep]
    for copy in wg_copies:
        copy.wait_recv()
    total = wg_buf[0]
    for k in range(1, n_rep):
        total = total + wg_buf[k]
    row_buf[row] = total
    for k in range(1, n_row):
        other = lax.rem(row + k, n_row)
        row_copies.append(pltpu.make_async_remote_copy(
            src_ref=row_buf.at[row], dst_ref=row_buf.at[row], send_sem=row_send.at[k], recv_sem=row_recv.at[k],
            device_id=(other, rep), device_id_type=MESH))
    for copy in row_copies:
        copy.start()
    for copy in ig_copies:
        copy.wait_recv()
    total = ig_buf[0]
    for k in range(1, n_rep):
        total = total + ig_buf[k]
    out_ref[...] = total.astype(out_ref.dtype)
    for copy in row_copies:
        copy.wait_recv()
    total = row_buf[0]
    for k in range(1, n_row):
        total = total + row_buf[k]
    full_buf[rep] = total
    for k in range(1, n_rep):
        other = lax.rem(rep + k, n_rep)
        full_copies.append(pltpu.make_async_remote_copy(
            src_ref=full_buf.at[rep], dst_ref=full_buf.at[rep], send_sem=full_send.at[k], recv_sem=full_recv.at[k],
            device_id=(row, other), device_id_type=MESH))
    for copy in full_copies:
        copy.start()
    for copy in full_copies:
        copy.wait_recv()
    wout_ref[...] = full_buf[...]
    for copy in wg_copies + ig_copies + row_copies + full_copies:
        copy.wait_send()


def reduce(ig_part, wg_part, n_row, n_rep):
    feats, hidden = wg_part.shape
    part = feats // n_rep
    rows_dev = ig_part.shape[0] * ig_part.shape[1] // n_rep
    width = ig_part.shape[2]
    vmem = pl.BlockSpec(memory_space=pltpu.VMEM)
    dma = pltpu.SemaphoreType.DMA
    out, wout = pl.pallas_call(
        functools.partial(reduce_kernel, n_row, n_rep),
        out_shape=(
            jax.ShapeDtypeStruct((rows_dev, width), jnp.bfloat16),
            jax.ShapeDtypeStruct((n_rep, part, hidden), jnp.float32),
        ),
        in_specs=[vmem, vmem],
        out_specs=(vmem, vmem),
        scratch_shapes=[
            pltpu.VMEM((n_rep, rows_dev, width), jnp.float32),
            pltpu.VMEM((n_rep, part, hidden), jnp.float32),
            pltpu.VMEM((n_row, part, hidden), jnp.float32),
            pltpu.VMEM((n_rep, part, hidden), jnp.float32),
            dma((n_rep,)), dma((n_rep,)), dma((n_rep,)), dma((n_rep,)),
            dma((n_row,)), dma((n_row,)), dma((n_rep,)), dma((n_rep,)),
        ],
        compiler_params=pltpu.CompilerParams(collective_id=1, has_side_effects=True, vmem_limit_bytes=32 * 2**20),
        name="reduce_grads",
    )(ig_part.reshape(n_rep, rows_dev, width), wg_part.reshape(n_rep, part, hidden))
    return out, wout.reshape(feats, hidden)


def on_device(features, grad_out, weight, tile_vals, tile_rows, tile_cols, tile_counts):
    n_row, n_rep = lax.axis_size("row"), lax.axis_size("rep")
    offsets = tile_vals.shape[2]
    gall, fall = gather(grad_out, features, n_row, n_rep, offsets)
    ig_part, wg_part = tile_products(tile_rows, tile_cols, tile_counts, tile_vals, gall, fall, weight)
    return reduce(ig_part, wg_part, n_row, n_rep)


def solution(mesh):
    placed = (
        P(("row", "rep"), None),
        P(("row", "rep"), None),
        P(),
        P("row", "rep", None, None, None, None),
        P("row", "rep", None, None),
        P("row", "rep", None, None),
        P("row", "rep", None),
    )
    return jax.shard_map(
        on_device,
        mesh=mesh,
        in_specs=placed,
        out_specs=(P(("row", "rep"), None), P()),
        check_vma=False,
    )
```

```python
import functools

import jax
import jax.numpy as jnp
from jax import lax
from jax.experimental import pallas as pl
from jax.experimental.pallas import tpu as pltpu
from jax.sharding import PartitionSpec as P

MESH = pl.DeviceIdType.MESH
GROUP = 8


def in_hbm(value):
    return pltpu.with_memory_space_constraint(value, pltpu.HBM)


def gather_kernel(n_row, n_rep, offsets, chain, g_ref, f_ref, weight_in, vals_in, gall_ref, fall_ref, weight_ref, vals_ref, send_sem, recv_sem, fsend_sem, frecv_sem, local_sem, vals_sem):
    row, rep = lax.axis_index("row"), lax.axis_index("rep")
    barrier = pltpu.get_barrier_semaphore()
    loads = [
        pltpu.make_async_copy(g_ref, gall_ref.at[row], local_sem.at[0]),
        pltpu.make_async_copy(f_ref, fall_ref.at[rep], local_sem.at[1]),
        pltpu.make_async_copy(weight_in, weight_ref, local_sem.at[2]),
    ]
    for s in range(offsets):
        loads.append(pltpu.make_async_copy(vals_in.at[0, 0, s], vals_ref.at[s], vals_sem.at[s]))

    def piece_copy(way, origin, half, target, own):
        return pltpu.make_async_remote_copy(
            src_ref=g_ref.at[half] if own else gall_ref.at[origin, half],
            dst_ref=gall_ref.at[origin, half],
            send_sem=send_sem.at[way, origin, half],
            recv_sem=recv_sem.at[origin, half],
            device_id=(target, rep), device_id_type=MESH)

    for k in range(1, n_rep):
        pl.semaphore_signal(barrier, inc=1, device_id=(row, lax.rem(rep + k, n_rep)), device_id_type=MESH)
    if chain:
        z, y = row // 2, row % 2
        length = n_row // 2
        beside, above, below = row + 1 - 2 * y, row + 2, row - 2
        has_above, has_below = z < length - 1, z > 0
        pl.semaphore_signal(barrier, inc=1, device_id=(beside, rep), device_id_type=MESH)

        @pl.when(has_above)
        def _():
            pl.semaphore_signal(barrier, inc=1, device_id=(above, rep), device_id_type=MESH)

        @pl.when(has_below)
        def _():
            pl.semaphore_signal(barrier, inc=1, device_id=(below, rep), device_id_type=MESH)

        pl.semaphore_wait(barrier, n_rep + has_above.astype(jnp.int32) + has_below.astype(jnp.int32))
    else:
        shifts = sorted({k % n_row for k in range(1, offsets)} | {-k % n_row for k in range(1, offsets)})
        for k in shifts:
            pl.semaphore_signal(barrier, inc=1, device_id=(lax.rem(row + k, n_row), rep), device_id_type=MESH)
        pl.semaphore_wait(barrier, len(shifts) + n_rep - 1)

    feat_copies = []
    for k in range(1, n_rep):
        feat_copies.append(pltpu.make_async_remote_copy(
            src_ref=f_ref, dst_ref=fall_ref.at[rep], send_sem=fsend_sem.at[k], recv_sem=frecv_sem.at[k],
            device_id=(row, lax.rem(rep + k, n_rep)), device_id_type=MESH))

    def start_rest():
        for copy in feat_copies:
            copy.start()
        for load in loads:
            load.start()
        gall_ref[n_row] = jnp.zeros(gall_ref.shape[1:], gall_ref.dtype)

    if chain:
        def send(cond, way, origin, half, target, own=False):
            pl.when(cond)(piece_copy(way, origin, half, target, own).start)

        always = row >= 0
        send(always, 0, row, 0, beside, True)
        send(has_above, 1, row, 1, above, True)
        send(has_below, 2, row, 1, below, True)
        send(has_above, 1, row, 0, above, True)
        send(has_below, 2, row, 0, below, True)
        send(always, 0, row, 1, beside, True)
        start_rest()
        piece_copy(0, beside, 0, beside, False).wait_recv()
        send(has_above, 1, beside, 0, above)
        send(has_below, 2, beside, 0, below)
        for dist in range(1, length):
            for down in (False, True):
                far = z + dist if down else z - dist
                there = far < length if down else far >= 0
                mine, other = far * 2 + y, far * 2 + 1 - y
                way, onward, target = (2, has_below, below) if down else (1, has_above, above)

                @pl.when(there)
                def _():
                    piece_copy(0, mine, 1, beside, False).wait_recv()
                    send(onward, way, mine, 1, target)
                    send(always, 0, mine, 1, beside)
                    piece_copy(0, mine, 0, beside, False).wait_recv()
                    send(onward, way, mine, 0, target)
                    piece_copy(0, other, 0, beside, False).wait_recv()
                    send(onward, way, other, 0, target)

        piece_copy(0, beside, 1, beside, False).wait_recv()
        for dist in range(1, length):
            for down in (False, True):
                far = z + dist if down else z - dist
                there = far < length if down else far >= 0
                other = far * 2 + 1 - y

                @pl.when(there)
                def _():
                    piece_copy(0, other, 1, beside, False).wait_recv()

        for load in loads:
            load.wait()
        for copy in feat_copies:
            copy.wait()
        for dist in range(length):
            for down in (False, True) if dist else (False,):
                far = z + dist if down else z - dist
                there = far < length if down else far >= 0
                mine, other = far * 2 + y, far * 2 + 1 - y
                outs = []
                if dist == 0:
                    outs += [(always, 0, mine, 0), (always, 0, mine, 1)]
                    for origin, half in ((mine, 0), (mine, 1), (other, 0)):
                        outs += [(has_above, 1, origin, half), (has_below, 2, origin, half)]
                else:
                    way, onward = (2, has_below) if down else (1, has_above)
                    outs += [(always, 0, mine, 1)]
                    outs += [(onward, way, origin, half) for origin, half in ((mine, 1), (mine, 0), (other, 0))]
                for cond, way, origin, half in outs:
                    copy = piece_copy(way, origin, half, beside, False)
                    pl.when(jnp.logical_and(there, cond))(copy.wait_send)
    else:
        copies = []
        for k in range(1, offsets):
            copies.append(pltpu.make_async_remote_copy(
                src_ref=g_ref, dst_ref=gall_ref.at[row], send_sem=send_sem.at[0, k, 0], recv_sem=recv_sem.at[k, 0],
                device_id=(lax.rem(row + k, n_row), rep), device_id_type=MESH))
        for copy in copies:
            copy.start()
        start_rest()
        for load in loads:
            load.wait()
        for copy in feat_copies + copies:
            copy.wait()


def gather(grad_out, features, weight, tile_vals, n_row, n_rep):
    offsets, slots, tile = tile_vals.shape[2:5]
    rows_dev, hidden = grad_out.shape
    chain = n_row == offsets and n_row % 2 == 0 and n_row >= 4 and rows_dev == 2 * tile
    vmem = pl.BlockSpec(memory_space=pltpu.VMEM)
    dma = pltpu.SemaphoreType.DMA
    return pl.pallas_call(
        functools.partial(gather_kernel, n_row, n_rep, offsets, chain),
        out_shape=(
            jax.ShapeDtypeStruct((n_row + 1, rows_dev // tile, tile, hidden), grad_out.dtype),
            jax.ShapeDtypeStruct((n_rep,) + features.shape, features.dtype),
            jax.ShapeDtypeStruct(weight.shape, weight.dtype),
            jax.ShapeDtypeStruct(tile_vals.shape[2:], tile_vals.dtype),
        ),
        in_specs=[pl.BlockSpec(memory_space=pltpu.HBM)] * 4,
        out_specs=(vmem,) * 4,
        scratch_shapes=[
            dma((3, n_row, 2)),
            dma((n_row, 2)),
            dma((n_rep,)),
            dma((n_rep,)),
            dma((3,)),
            dma((offsets,)),
        ],
        compiler_params=pltpu.CompilerParams(collective_id=0, has_side_effects=True, vmem_limit_bytes=24 * 2**20),
        name="gather_sources",
    )(*map(in_hbm, (grad_out.reshape(rows_dev // tile, tile, hidden), features, weight, tile_vals)))


def dot_first(left, right):
    return lax.dot_general(left, right, (((0,), (0,)), ((), ())), preferred_element_type=jnp.float32)


def split(value):
    high = value.astype(jnp.bfloat16)
    low = (value - high.astype(jnp.float32)).astype(jnp.bfloat16)
    return high, low


def tiles_kernel(offsets, tile, col_tiles, rows_in, cols_in, counts_in, vals, blocks, fall_ref, weight_ref, ig_ref, wg_ref, totals, rows_ref, cols_ref, counts_ref, sem):
    loads = [
        pltpu.make_async_copy(rows_in, rows_ref, sem.at[0]),
        pltpu.make_async_copy(cols_in, cols_ref, sem.at[1]),
        pltpu.make_async_copy(counts_in, counts_ref, sem.at[2]),
    ]
    for load in loads:
        load.start()
    totals[...] = jnp.zeros_like(totals)
    row, n_row = lax.axis_index("row"), lax.axis_size("row")
    for load in loads:
        load.wait()

    def one_offset(s, carry):
        count = counts_ref[0, 0, s]
        origin = lax.rem(row + n_row - s, n_row)

        def one_group(group, carry):
            parts = []
            for u in range(GROUP):
                k = group * GROUP + u
                chosen = blocks[jnp.where(k < count, origin, n_row), rows_ref[0, 0, s, k]]
                parts.append((cols_ref[0, 0, s, k], dot_first(vals[s, k], chosen)))
            for col, part in parts:
                totals[col] += part
            return carry

        return lax.fori_loop(0, (count + GROUP - 1) // GROUP, one_group, carry)

    lax.fori_loop(0, offsets, one_offset, 0)
    weight = weight_ref[...]
    feats, hidden = weight.shape

    def one_col(col, wg):
        high, low = split(totals[col])
        dims = (((1,), (1,)), ((), ()))
        ig_ref[col] = (
            lax.dot_general(high, weight, dims, preferred_element_type=jnp.float32)
            + lax.dot_general(low, weight, dims, preferred_element_type=jnp.float32))
        return wg + dot_first(fall_ref[col], high) + dot_first(fall_ref[col], low)

    wg = jnp.zeros((feats, hidden), jnp.float32)
    if col_tiles <= 8:
        for col in range(col_tiles):
            wg = one_col(col, wg)
    else:
        wg = lax.fori_loop(0, col_tiles, one_col, wg)
    for chunk in range(wg_ref.shape[0]):
        i, j = chunk // (hidden // 128), chunk % (hidden // 128)
        wg_ref[chunk] = wg[8 * i:8 * i + 8, 128 * j:128 * j + 128]


def tile_products(tile_rows, tile_cols, tile_counts, vals, gall, fall, weight):
    offsets, slots, tile = vals.shape[:3]
    row_tiles, hidden = gall.shape[1], gall.shape[3]
    n_rep, _, feats = fall.shape
    col_tiles = n_rep * row_tiles
    vmem = pl.BlockSpec(memory_space=pltpu.VMEM)
    hbm = pl.BlockSpec(memory_space=pltpu.HBM)
    return pl.pallas_call(
        functools.partial(tiles_kernel, offsets, tile, col_tiles),
        out_shape=(
            jax.ShapeDtypeStruct((col_tiles, tile, feats), jnp.float32),
            jax.ShapeDtypeStruct((feats * hidden // 1024, 8, 128), jnp.float32),
        ),
        in_specs=[hbm, hbm, hbm, vmem, vmem, vmem, vmem],
        out_specs=(vmem, vmem),
        scratch_shapes=[
            pltpu.VMEM((col_tiles, tile, hidden), jnp.float32),
            pltpu.SMEM(tile_rows.shape, jnp.int32),
            pltpu.SMEM(tile_cols.shape, jnp.int32),
            pltpu.SMEM(tile_counts.shape, jnp.int32),
            pltpu.SemaphoreType.DMA((3,)),
        ],
        compiler_params=pltpu.CompilerParams(vmem_limit_bytes=32 * 2**20),
        name="tile_products",
    )(in_hbm(tile_rows), in_hbm(tile_cols), in_hbm(tile_counts), vals, gall, fall.reshape(col_tiles, tile, feats), weight)


def reduce_kernel(n_row, n_rep, ig_ref, wg_ref, out_ref, wout_ref, pair_buf, mid_buf, ig_buf, wg_buf, row_buf, sum_buf, full_buf, pair_send, pair_recv, ig_send, ig_recv, wg_send, wg_recv, row_send, row_recv, sum_send, sum_recv, full_send, full_recv):
    row, rep = lax.axis_index("row"), lax.axis_index("rep")
    pairs = n_rep // 2
    pair, core = rep // 2, rep % 2
    chunks = wg_ref.shape[1]
    scatter = chunks % n_row == 0
    share = chunks // n_row if scatter else chunks
    barrier = pltpu.get_barrier_semaphore()
    for k in range(1, n_row):
        pl.semaphore_signal(barrier, inc=1, device_id=(lax.rem(row + k, n_row), rep), device_id_type=MESH)
    for k in range(1, n_rep):
        pl.semaphore_signal(barrier, inc=1, device_id=(row, lax.rem(rep + k, n_rep)), device_id_type=MESH)
    pl.semaphore_wait(barrier, n_row + n_rep - 2)

    started = []

    def copy_to(src, dst, send, recv, target):
        copy = pltpu.make_async_remote_copy(
            src_ref=src, dst_ref=dst, send_sem=send, recv_sem=recv, device_id=target, device_id_type=MESH)
        copy.start()
        started.append(copy)
        return copy

    wg_copies, pair_copies, ig_copies, row_copies, sum_copies, full_copies = [], [], [], [], [], []
    for k in range(1, n_rep):
        other = lax.rem(rep + k, n_rep)
        wg_copies.append(copy_to(wg_ref.at[other], wg_buf.at[rep], wg_send.at[k], wg_recv.at[k], (row, other)))
    for k in range(1, pairs + 1):
        block = lax.rem(pair + k, pairs)
        pair_copies.append(copy_to(
            ig_ref.at[block * 2 + 1 - core], pair_buf.at[block], pair_send.at[k - 1], pair_recv.at[k - 1],
            (row, rep + 1 - 2 * core)))
    for k in range(1, pairs):
        block = lax.rem(pair + k, pairs)
        pair_copies[k - 1].wait_recv()
        mid_buf[block] = ig_ref[block * 2 + core] + pair_buf[block]
        ig_copies.append(copy_to(
            mid_buf.at[block], ig_buf.at[pair], ig_send.at[k], ig_recv.at[k], (row, block * 2 + core)))
    wg_buf[rep] = wg_ref[rep]
    for copy in wg_copies:
        copy.wait_recv()
    total = wg_buf[0]
    for k in range(1, n_rep):
        total = total + wg_buf[k]
    sum_buf[...] = total.reshape(sum_buf.shape)
    for k in range(1, n_row):
        other = lax.rem(row + k, n_row)
        source = sum_buf.at[other] if scatter else sum_buf.at[0]
        row_copies.append(copy_to(source, row_buf.at[row], row_send.at[k], row_recv.at[k], (other, rep)))
    row_buf[row] = sum_buf[row] if scatter else sum_buf[0]
    for copy in row_copies:
        copy.wait_recv()
    total = row_buf[0]
    for k in range(1, n_row):
        total = total + row_buf[k]
    if scatter:
        full_buf[rep, row] = total
        for k in range(1, n_row):
            other = lax.rem(row + k, n_row)
            sum_copies.append(copy_to(
                full_buf.at[rep, row], full_buf.at[rep, row], sum_send.at[k], sum_recv.at[k], (other, rep)))
        for copy in sum_copies:
            copy.wait_recv()
    else:
        full_buf[rep, 0] = total
    for k in range(1, n_rep):
        other = lax.rem(rep + k, n_rep)
        full_copies.append(copy_to(
            full_buf.at[rep], full_buf.at[rep], full_send.at[k], full_recv.at[k], (row, other)))
    pair_copies[pairs - 1].wait_recv()
    total = ig_ref[rep] + pair_buf[pair]
    for k in range(1, pairs):
        ig_copies[k - 1].wait_recv()
        total = total + ig_buf[lax.rem(pair - k + pairs, pairs)]
    out_ref[...] = total.astype(out_ref.dtype)
    for copy in full_copies:
        copy.wait_recv()
    across = wout_ref.shape[1] // 128
    full = full_buf[...].reshape((n_rep * chunks, 8, 128))
    for chunk in range(n_rep * chunks):
        i, j = chunk // across, chunk % across
        wout_ref[8 * i:8 * i + 8, 128 * j:128 * j + 128] = full[chunk]
    for copy in started:
        copy.wait_send()


def reduce(ig_part, wg_part, feats, hidden, n_row, n_rep):
    chunks = wg_part.shape[0] // n_rep
    scatter = chunks % n_row == 0
    owners = n_row if scatter else 1
    share = chunks // owners
    rows_dev = ig_part.shape[0] * ig_part.shape[1] // n_rep
    width = ig_part.shape[2]
    pairs = n_rep // 2
    vmem = pl.BlockSpec(memory_space=pltpu.VMEM)
    dma = pltpu.SemaphoreType.DMA
    return pl.pallas_call(
        functools.partial(reduce_kernel, n_row, n_rep),
        out_shape=(
            jax.ShapeDtypeStruct((rows_dev, width), jnp.bfloat16),
            jax.ShapeDtypeStruct((feats, hidden), jnp.float32),
        ),
        in_specs=[vmem, vmem],
        out_specs=(vmem, vmem),
        scratch_shapes=[
            pltpu.VMEM((pairs, rows_dev, width), jnp.float32),
            pltpu.VMEM((pairs, rows_dev, width), jnp.float32),
            pltpu.VMEM((pairs, rows_dev, width), jnp.float32),
            pltpu.VMEM((n_rep, chunks, 8, 128), jnp.float32),
            pltpu.VMEM((n_row, share, 8, 128), jnp.float32),
            pltpu.VMEM((owners, share, 8, 128), jnp.float32),
            pltpu.VMEM((n_rep, owners, share, 8, 128), jnp.float32),
            dma((pairs,)), dma((pairs,)), dma((pairs,)), dma((pairs,)),
            dma((n_rep,)), dma((n_rep,)), dma((n_row,)), dma((n_row,)),
            dma((n_row,)), dma((n_row,)), dma((n_rep,)), dma((n_rep,)),
        ],
        compiler_params=pltpu.CompilerParams(collective_id=1, has_side_effects=True, vmem_limit_bytes=32 * 2**20),
        name="reduce_grads",
    )(ig_part.reshape(n_rep, rows_dev, width), wg_part.reshape(n_rep, chunks, 8, 128))


def on_device(features, grad_out, weight, tile_vals, tile_rows, tile_cols, tile_counts):
    n_row, n_rep = lax.axis_size("row"), lax.axis_size("rep")
    gall, fall, weight_near, vals = gather(grad_out, features, weight, tile_vals, n_row, n_rep)
    ig_part, wg_part = tile_products(tile_rows, tile_cols, tile_counts, vals, gall, fall, weight_near)
    return reduce(ig_part, wg_part, weight.shape[0], weight.shape[1], n_row, n_rep)


def solution(mesh):
    placed = (
        P(("row", "rep"), None),
        P(("row", "rep"), None),
        P(),
        P("row", "rep", None, None, None, None),
        P("row", "rep", None, None),
        P("row", "rep", None, None),
        P("row", "rep", None),
    )
    return jax.shard_map(
        on_device,
        mesh=mesh,
        in_specs=placed,
        out_specs=(P(("row", "rep"), None), P()),
        check_vma=False,
    )
```

```python
import functools

import jax
import jax.numpy as jnp
from jax import lax
from jax.experimental import pallas as pl
from jax.experimental.pallas import tpu as pltpu
from jax.sharding import PartitionSpec as P

MESH = pl.DeviceIdType.MESH
GROUP = 40


def in_hbm(value):
    return pltpu.with_memory_space_constraint(value, pltpu.HBM)


def gather_kernel(n_row, n_rep, offsets, chain, g_ref, f_ref, weight_in, vals_in, gall_ref, fall_ref, weight_ref, vals_ref, send_sem, recv_sem, fsend_sem, frecv_sem, local_sem, vals_sem):
    row, rep = lax.axis_index("row"), lax.axis_index("rep")
    barrier = pltpu.get_barrier_semaphore()
    loads = [
        pltpu.make_async_copy(g_ref, gall_ref.at[row], local_sem.at[0]),
        pltpu.make_async_copy(f_ref, fall_ref.at[rep], local_sem.at[1]),
        pltpu.make_async_copy(weight_in, weight_ref, local_sem.at[2]),
    ]
    for s in range(offsets):
        loads.append(pltpu.make_async_copy(vals_in.at[0, 0, s], vals_ref.at[s], vals_sem.at[s]))

    def piece_copy(way, origin, half, target, own):
        return pltpu.make_async_remote_copy(
            src_ref=g_ref.at[half] if own else gall_ref.at[origin, half],
            dst_ref=gall_ref.at[origin, half],
            send_sem=send_sem.at[way, origin, half],
            recv_sem=recv_sem.at[origin, half],
            device_id=(target, rep), device_id_type=MESH)

    for k in range(1, n_rep):
        pl.semaphore_signal(barrier, inc=1, device_id=(row, lax.rem(rep + k, n_rep)), device_id_type=MESH)
    if chain:
        z, y = row // 2, row % 2
        length = n_row // 2
        beside, above, below = row + 1 - 2 * y, row + 2, row - 2
        has_above, has_below = z < length - 1, z > 0
        pl.semaphore_signal(barrier, inc=1, device_id=(beside, rep), device_id_type=MESH)

        @pl.when(has_above)
        def _():
            pl.semaphore_signal(barrier, inc=1, device_id=(above, rep), device_id_type=MESH)

        @pl.when(has_below)
        def _():
            pl.semaphore_signal(barrier, inc=1, device_id=(below, rep), device_id_type=MESH)

        pl.semaphore_wait(barrier, n_rep + has_above.astype(jnp.int32) + has_below.astype(jnp.int32))
    else:
        shifts = sorted({k % n_row for k in range(1, offsets)} | {-k % n_row for k in range(1, offsets)})
        for k in shifts:
            pl.semaphore_signal(barrier, inc=1, device_id=(lax.rem(row + k, n_row), rep), device_id_type=MESH)
        pl.semaphore_wait(barrier, len(shifts) + n_rep - 1)

    feat_copies = []
    for k in range(1, n_rep):
        feat_copies.append(pltpu.make_async_remote_copy(
            src_ref=f_ref, dst_ref=fall_ref.at[rep], send_sem=fsend_sem.at[k], recv_sem=frecv_sem.at[k],
            device_id=(row, lax.rem(rep + k, n_rep)), device_id_type=MESH))

    def start_rest():
        for copy in feat_copies:
            copy.start()
        for load in loads:
            load.start()
        gall_ref[n_row] = jnp.zeros(gall_ref.shape[1:], gall_ref.dtype)

    if chain:
        def send(cond, way, origin, half, target, own=False):
            pl.when(cond)(piece_copy(way, origin, half, target, own).start)

        always = row >= 0
        send(always, 0, row, 0, beside, True)
        send(has_above, 1, row, 1, above, True)
        send(has_below, 2, row, 1, below, True)
        send(has_above, 1, row, 0, above, True)
        send(has_below, 2, row, 0, below, True)
        send(always, 0, row, 1, beside, True)
        start_rest()
        piece_copy(0, beside, 0, beside, False).wait_recv()
        send(has_above, 1, beside, 0, above)
        send(has_below, 2, beside, 0, below)
        for dist in range(1, length):
            for down in (False, True):
                far = z + dist if down else z - dist
                there = far < length if down else far >= 0
                mine, other = far * 2 + y, far * 2 + 1 - y
                way, onward, target = (2, has_below, below) if down else (1, has_above, above)

                @pl.when(there)
                def _():
                    piece_copy(0, mine, 1, beside, False).wait_recv()
                    send(onward, way, mine, 1, target)
                    send(always, 0, mine, 1, beside)
                    piece_copy(0, mine, 0, beside, False).wait_recv()
                    send(onward, way, mine, 0, target)
                    piece_copy(0, other, 0, beside, False).wait_recv()
                    send(onward, way, other, 0, target)

        piece_copy(0, beside, 1, beside, False).wait_recv()
        for dist in range(1, length):
            for down in (False, True):
                far = z + dist if down else z - dist
                there = far < length if down else far >= 0
                other = far * 2 + 1 - y

                @pl.when(there)
                def _():
                    piece_copy(0, other, 1, beside, False).wait_recv()

        for load in loads:
            load.wait()
        for copy in feat_copies:
            copy.wait()
        for dist in range(length):
            for down in (False, True) if dist else (False,):
                far = z + dist if down else z - dist
                there = far < length if down else far >= 0
                mine, other = far * 2 + y, far * 2 + 1 - y
                outs = []
                if dist == 0:
                    outs += [(always, 0, mine, 0), (always, 0, mine, 1)]
                    for origin, half in ((mine, 0), (mine, 1), (other, 0)):
                        outs += [(has_above, 1, origin, half), (has_below, 2, origin, half)]
                else:
                    way, onward = (2, has_below) if down else (1, has_above)
                    outs += [(always, 0, mine, 1)]
                    outs += [(onward, way, origin, half) for origin, half in ((mine, 1), (mine, 0), (other, 0))]
                for cond, way, origin, half in outs:
                    copy = piece_copy(way, origin, half, beside, False)
                    pl.when(jnp.logical_and(there, cond))(copy.wait_send)
    else:
        copies = []
        for k in range(1, offsets):
            copies.append(pltpu.make_async_remote_copy(
                src_ref=g_ref, dst_ref=gall_ref.at[row], send_sem=send_sem.at[0, k, 0], recv_sem=recv_sem.at[k, 0],
                device_id=(lax.rem(row + k, n_row), rep), device_id_type=MESH))
        for copy in copies:
            copy.start()
        start_rest()
        for load in loads:
            load.wait()
        for copy in feat_copies + copies:
            copy.wait()


def gather(grad_out, features, weight, tile_vals, n_row, n_rep):
    offsets, slots, tile = tile_vals.shape[2:5]
    rows_dev, hidden = grad_out.shape
    chain = n_row == offsets and n_row % 2 == 0 and n_row >= 4 and rows_dev == 2 * tile
    vmem = pl.BlockSpec(memory_space=pltpu.VMEM)
    dma = pltpu.SemaphoreType.DMA
    return pl.pallas_call(
        functools.partial(gather_kernel, n_row, n_rep, offsets, chain),
        out_shape=(
            jax.ShapeDtypeStruct((n_row + 1, rows_dev // tile, tile, hidden), grad_out.dtype),
            jax.ShapeDtypeStruct((n_rep,) + features.shape, features.dtype),
            jax.ShapeDtypeStruct(weight.shape, weight.dtype),
            jax.ShapeDtypeStruct(tile_vals.shape[2:], tile_vals.dtype),
        ),
        in_specs=[pl.BlockSpec(memory_space=pltpu.HBM)] * 4,
        out_specs=(vmem,) * 4,
        scratch_shapes=[
            dma((3, n_row, 2)),
            dma((n_row, 2)),
            dma((n_rep,)),
            dma((n_rep,)),
            dma((3,)),
            dma((offsets,)),
        ],
        compiler_params=pltpu.CompilerParams(collective_id=0, has_side_effects=True, vmem_limit_bytes=24 * 2**20),
        name="gather_sources",
    )(*map(in_hbm, (grad_out.reshape(rows_dev // tile, tile, hidden), features, weight, tile_vals)))


def dot_first(left, right):
    return lax.dot_general(left, right, (((0,), (0,)), ((), ())), preferred_element_type=jnp.float32)


def split(value):
    high = value.astype(jnp.bfloat16)
    low = (value - high.astype(jnp.float32)).astype(jnp.bfloat16)
    return high, low


def tiles_kernel(offsets, tile, col_tiles, rows_in, cols_in, counts_in, vals, blocks, fall_ref, weight_ref, ig_ref, wg_ref, totals, rows_ref, cols_ref, counts_ref, sem):
    loads = [
        pltpu.make_async_copy(rows_in, rows_ref, sem.at[0]),
        pltpu.make_async_copy(cols_in, cols_ref, sem.at[1]),
        pltpu.make_async_copy(counts_in, counts_ref, sem.at[2]),
    ]
    for load in loads:
        load.start()
    totals[...] = jnp.zeros_like(totals)
    row, n_row = lax.axis_index("row"), lax.axis_size("row")
    for load in loads:
        load.wait()

    def one_offset(s, carry):
        count = counts_ref[0, 0, s]
        origin = lax.rem(row + n_row - s, n_row)

        def one_group(group, carry):
            parts = []
            for u in range(GROUP):
                k = group * GROUP + u
                chosen = blocks[jnp.where(k < count, origin, n_row), rows_ref[0, 0, s, k]]
                parts.append((cols_ref[0, 0, s, k], dot_first(vals[s, k], chosen)))
            for col, part in parts:
                totals[col] += part
            return carry

        return lax.fori_loop(0, (count + GROUP - 1) // GROUP, one_group, carry)

    lax.fori_loop(0, offsets, one_offset, 0)
    weight = weight_ref[...]
    feats, hidden = weight.shape

    def one_col(col, wg):
        high, low = split(totals[col])
        dims = (((1,), (1,)), ((), ()))
        ig_ref[col] = (
            lax.dot_general(high, weight, dims, preferred_element_type=jnp.float32)
            + lax.dot_general(low, weight, dims, preferred_element_type=jnp.float32))
        return wg + dot_first(fall_ref[col], high) + dot_first(fall_ref[col], low)

    wg = jnp.zeros((feats, hidden), jnp.float32)
    if col_tiles <= 8:
        for col in range(col_tiles):
            wg = one_col(col, wg)
    else:
        wg = lax.fori_loop(0, col_tiles, one_col, wg)
    for chunk in range(wg_ref.shape[0]):
        i, j = chunk // (hidden // 128), chunk % (hidden // 128)
        wg_ref[chunk] = wg[8 * i:8 * i + 8, 128 * j:128 * j + 128]


def tile_products(tile_rows, tile_cols, tile_counts, vals, gall, fall, weight):
    offsets, slots, tile = vals.shape[:3]
    row_tiles, hidden = gall.shape[1], gall.shape[3]
    n_rep, _, feats = fall.shape
    col_tiles = n_rep * row_tiles
    vmem = pl.BlockSpec(memory_space=pltpu.VMEM)
    hbm = pl.BlockSpec(memory_space=pltpu.HBM)
    return pl.pallas_call(
        functools.partial(tiles_kernel, offsets, tile, col_tiles),
        out_shape=(
            jax.ShapeDtypeStruct((col_tiles, tile, feats), jnp.float32),
            jax.ShapeDtypeStruct((feats * hidden // 1024, 8, 128), jnp.float32),
        ),
        in_specs=[hbm, hbm, hbm, vmem, vmem, vmem, vmem],
        out_specs=(vmem, vmem),
        scratch_shapes=[
            pltpu.VMEM((col_tiles, tile, hidden), jnp.float32),
            pltpu.SMEM(tile_rows.shape, jnp.int32),
            pltpu.SMEM(tile_cols.shape, jnp.int32),
            pltpu.SMEM(tile_counts.shape, jnp.int32),
            pltpu.SemaphoreType.DMA((3,)),
        ],
        compiler_params=pltpu.CompilerParams(vmem_limit_bytes=32 * 2**20),
        name="tile_products",
    )(in_hbm(tile_rows), in_hbm(tile_cols), in_hbm(tile_counts), vals, gall, fall.reshape(col_tiles, tile, feats), weight)


def reduce_kernel(n_row, n_rep, ig_ref, wg_ref, out_ref, wout_ref, pair_buf, mid_buf, ig_buf, wg_buf, row_buf, sum_buf, full_buf, pair_send, pair_recv, ig_send, ig_recv, wg_send, wg_recv, row_send, row_recv, sum_send, sum_recv, full_send, full_recv):
    row, rep = lax.axis_index("row"), lax.axis_index("rep")
    pairs = n_rep // 2
    pair, core = rep // 2, rep % 2
    chunks = wg_ref.shape[1]
    scatter = chunks % n_row == 0
    share = chunks // n_row if scatter else chunks
    barrier = pltpu.get_barrier_semaphore()
    for k in range(1, n_row):
        pl.semaphore_signal(barrier, inc=1, device_id=(lax.rem(row + k, n_row), rep), device_id_type=MESH)
    for k in range(1, n_rep):
        pl.semaphore_signal(barrier, inc=1, device_id=(row, lax.rem(rep + k, n_rep)), device_id_type=MESH)
    pl.semaphore_wait(barrier, n_row + n_rep - 2)

    started = []

    def copy_to(src, dst, send, recv, target):
        copy = pltpu.make_async_remote_copy(
            src_ref=src, dst_ref=dst, send_sem=send, recv_sem=recv, device_id=target, device_id_type=MESH)
        copy.start()
        started.append(copy)
        return copy

    wg_copies, pair_copies, ig_copies, row_copies, sum_copies, full_copies = [], [], [], [], [], []
    for k in range(1, n_rep):
        other = lax.rem(rep + k, n_rep)
        wg_copies.append(copy_to(wg_ref.at[other], wg_buf.at[rep], wg_send.at[k], wg_recv.at[k], (row, other)))
    for k in range(1, pairs + 1):
        block = lax.rem(pair + k, pairs)
        pair_copies.append(copy_to(
            ig_ref.at[block * 2 + 1 - core], pair_buf.at[block], pair_send.at[k - 1], pair_recv.at[k - 1],
            (row, rep + 1 - 2 * core)))
    for k in range(1, pairs):
        block = lax.rem(pair + k, pairs)
        pair_copies[k - 1].wait_recv()
        mid_buf[block] = ig_ref[block * 2 + core] + pair_buf[block]
        ig_copies.append(copy_to(
            mid_buf.at[block], ig_buf.at[pair], ig_send.at[k], ig_recv.at[k], (row, block * 2 + core)))
    wg_buf[rep] = wg_ref[rep]
    for copy in wg_copies:
        copy.wait_recv()
    total = wg_buf[0]
    for k in range(1, n_rep):
        total = total + wg_buf[k]
    sum_buf[...] = total.reshape(sum_buf.shape)
    for k in range(1, n_row):
        other = lax.rem(row + k, n_row)
        source = sum_buf.at[other] if scatter else sum_buf.at[0]
        row_copies.append(copy_to(source, row_buf.at[row], row_send.at[k], row_recv.at[k], (other, rep)))
    row_buf[row] = sum_buf[row] if scatter else sum_buf[0]
    for copy in row_copies:
        copy.wait_recv()
    total = row_buf[0]
    for k in range(1, n_row):
        total = total + row_buf[k]
    if scatter:
        full_buf[rep, row] = total
        for k in range(1, n_row):
            other = lax.rem(row + k, n_row)
            sum_copies.append(copy_to(
                full_buf.at[rep, row], full_buf.at[rep, row], sum_send.at[k], sum_recv.at[k], (other, rep)))
        for copy in sum_copies:
            copy.wait_recv()
    else:
        full_buf[rep, 0] = total
    for k in range(1, n_rep):
        other = lax.rem(rep + k, n_rep)
        full_copies.append(copy_to(
            full_buf.at[rep], full_buf.at[rep], full_send.at[k], full_recv.at[k], (row, other)))
    pair_copies[pairs - 1].wait_recv()
    total = ig_ref[rep] + pair_buf[pair]
    for k in range(1, pairs):
        ig_copies[k - 1].wait_recv()
        total = total + ig_buf[lax.rem(pair - k + pairs, pairs)]
    out_ref[...] = total.astype(out_ref.dtype)
    for copy in full_copies:
        copy.wait_recv()
    across = wout_ref.shape[1] // 128
    full = full_buf[...].reshape((n_rep * chunks, 8, 128))
    for chunk in range(n_rep * chunks):
        i, j = chunk // across, chunk % across
        wout_ref[8 * i:8 * i + 8, 128 * j:128 * j + 128] = full[chunk]
    for copy in started:
        copy.wait_send()


def reduce(ig_part, wg_part, feats, hidden, n_row, n_rep):
    chunks = wg_part.shape[0] // n_rep
    scatter = chunks % n_row == 0
    owners = n_row if scatter else 1
    share = chunks // owners
    rows_dev = ig_part.shape[0] * ig_part.shape[1] // n_rep
    width = ig_part.shape[2]
    pairs = n_rep // 2
    vmem = pl.BlockSpec(memory_space=pltpu.VMEM)
    dma = pltpu.SemaphoreType.DMA
    return pl.pallas_call(
        functools.partial(reduce_kernel, n_row, n_rep),
        out_shape=(
            jax.ShapeDtypeStruct((rows_dev, width), jnp.bfloat16),
            jax.ShapeDtypeStruct((feats, hidden), jnp.float32),
        ),
        in_specs=[vmem, vmem],
        out_specs=(vmem, vmem),
        scratch_shapes=[
            pltpu.VMEM((pairs, rows_dev, width), jnp.float32),
            pltpu.VMEM((pairs, rows_dev, width), jnp.float32),
            pltpu.VMEM((pairs, rows_dev, width), jnp.float32),
            pltpu.VMEM((n_rep, chunks, 8, 128), jnp.float32),
            pltpu.VMEM((n_row, share, 8, 128), jnp.float32),
            pltpu.VMEM((owners, share, 8, 128), jnp.float32),
            pltpu.VMEM((n_rep, owners, share, 8, 128), jnp.float32),
            dma((pairs,)), dma((pairs,)), dma((pairs,)), dma((pairs,)),
            dma((n_rep,)), dma((n_rep,)), dma((n_row,)), dma((n_row,)),
            dma((n_row,)), dma((n_row,)), dma((n_rep,)), dma((n_rep,)),
        ],
        compiler_params=pltpu.CompilerParams(collective_id=1, has_side_effects=True, vmem_limit_bytes=32 * 2**20),
        name="reduce_grads",
    )(ig_part.reshape(n_rep, rows_dev, width), wg_part.reshape(n_rep, chunks, 8, 128))


def on_device(features, grad_out, weight, tile_vals, tile_rows, tile_cols, tile_counts):
    n_row, n_rep = lax.axis_size("row"), lax.axis_size("rep")
    gall, fall, weight_near, vals = gather(grad_out, features, weight, tile_vals, n_row, n_rep)
    ig_part, wg_part = tile_products(tile_rows, tile_cols, tile_counts, vals, gall, fall, weight_near)
    return reduce(ig_part, wg_part, weight.shape[0], weight.shape[1], n_row, n_rep)


def solution(mesh):
    placed = (
        P(("row", "rep"), None),
        P(("row", "rep"), None),
        P(),
        P("row", "rep", None, None, None, None),
        P("row", "rep", None, None),
        P("row", "rep", None, None),
        P("row", "rep", None),
    )
    return jax.shard_map(
        on_device,
        mesh=mesh,
        in_specs=placed,
        out_specs=(P(("row", "rep"), None), P()),
        check_vma=False,
    )
```

```python
import functools

import jax
import jax.numpy as jnp
from jax import lax
from jax.experimental import pallas as pl
from jax.experimental.pallas import tpu as pltpu
from jax.sharding import PartitionSpec as P

MESH = pl.DeviceIdType.MESH
GROUP = 40


def in_hbm(value):
    return pltpu.with_memory_space_constraint(value, pltpu.HBM)


def gather_kernel(n_row, n_rep, offsets, chain, g_ref, f_ref, weight_in, vals_in, gall_ref, fall_ref, weight_ref, vals_ref, send_sem, recv_sem, fsend_sem, frecv_sem, local_sem, vals_sem):
    row, rep = lax.axis_index("row"), lax.axis_index("rep")
    barrier = pltpu.get_barrier_semaphore()
    loads = [
        pltpu.make_async_copy(g_ref, gall_ref.at[row], local_sem.at[0]),
        pltpu.make_async_copy(f_ref, fall_ref.at[rep], local_sem.at[1]),
        pltpu.make_async_copy(weight_in, weight_ref, local_sem.at[2]),
    ]
    for s in range(offsets):
        loads.append(pltpu.make_async_copy(vals_in.at[0, 0, s], vals_ref.at[s], vals_sem.at[s]))

    for load in loads:
        load.start()

    def piece_copy(way, origin, half, target, own):
        return pltpu.make_async_remote_copy(
            src_ref=g_ref.at[half] if own else gall_ref.at[origin, half],
            dst_ref=gall_ref.at[origin, half],
            send_sem=send_sem.at[way, origin, half],
            recv_sem=recv_sem.at[origin, half],
            device_id=(target, rep), device_id_type=MESH)

    for k in range(1, n_rep):
        pl.semaphore_signal(barrier, inc=1, device_id=(row, lax.rem(rep + k, n_rep)), device_id_type=MESH)
    if chain:
        z, y = row // 2, row % 2
        length = n_row // 2
        beside, above, below = row + 1 - 2 * y, row + 2, row - 2
        has_above, has_below = z < length - 1, z > 0
        pl.semaphore_signal(barrier, inc=1, device_id=(beside, rep), device_id_type=MESH)

        @pl.when(has_above)
        def _():
            pl.semaphore_signal(barrier, inc=1, device_id=(above, rep), device_id_type=MESH)

        @pl.when(has_below)
        def _():
            pl.semaphore_signal(barrier, inc=1, device_id=(below, rep), device_id_type=MESH)

        pl.semaphore_wait(barrier, n_rep + has_above.astype(jnp.int32) + has_below.astype(jnp.int32))
    else:
        shifts = sorted({k % n_row for k in range(1, offsets)} | {-k % n_row for k in range(1, offsets)})
        for k in shifts:
            pl.semaphore_signal(barrier, inc=1, device_id=(lax.rem(row + k, n_row), rep), device_id_type=MESH)
        pl.semaphore_wait(barrier, len(shifts) + n_rep - 1)

    feat_copies = []
    for k in range(1, n_rep):
        feat_copies.append(pltpu.make_async_remote_copy(
            src_ref=f_ref, dst_ref=fall_ref.at[rep], send_sem=fsend_sem.at[k], recv_sem=frecv_sem.at[k],
            device_id=(row, lax.rem(rep + k, n_rep)), device_id_type=MESH))

    def start_rest():
        for copy in feat_copies:
            copy.start()
        gall_ref[n_row] = jnp.zeros(gall_ref.shape[1:], gall_ref.dtype)

    if chain:
        def send(cond, way, origin, half, target, own=False):
            pl.when(cond)(piece_copy(way, origin, half, target, own).start)

        always = row >= 0
        send(always, 0, row, 0, beside, True)
        send(has_above, 1, row, 1, above, True)
        send(has_below, 2, row, 1, below, True)
        send(has_above, 1, row, 0, above, True)
        send(has_below, 2, row, 0, below, True)
        send(always, 0, row, 1, beside, True)
        start_rest()
        piece_copy(0, beside, 0, beside, False).wait_recv()
        send(has_above, 1, beside, 0, above)
        send(has_below, 2, beside, 0, below)
        for dist in range(1, length):
            for item in range(3):
                for down in (False, True):
                    far = z + dist if down else z - dist
                    there = far < length if down else far >= 0
                    origin = far * 2 + (1 - y if item == 2 else y)
                    half = 1 if item == 0 else 0
                    way, onward, target = (2, has_below, below) if down else (1, has_above, above)

                    @pl.when(there)
                    def _():
                        piece_copy(0, origin, half, beside, False).wait_recv()
                        send(onward, way, origin, half, target)
                        if item == 0:
                            send(always, 0, origin, half, beside)

        piece_copy(0, beside, 1, beside, False).wait_recv()
        for dist in range(1, length):
            for down in (False, True):
                far = z + dist if down else z - dist
                there = far < length if down else far >= 0
                other = far * 2 + 1 - y

                @pl.when(there)
                def _():
                    piece_copy(0, other, 1, beside, False).wait_recv()

        for load in loads:
            load.wait()
        for copy in feat_copies:
            copy.wait()
        for dist in range(length):
            for down in (False, True) if dist else (False,):
                far = z + dist if down else z - dist
                there = far < length if down else far >= 0
                mine, other = far * 2 + y, far * 2 + 1 - y
                outs = []
                if dist == 0:
                    outs += [(always, 0, mine, 0), (always, 0, mine, 1)]
                    for origin, half in ((mine, 0), (mine, 1), (other, 0)):
                        outs += [(has_above, 1, origin, half), (has_below, 2, origin, half)]
                else:
                    way, onward = (2, has_below) if down else (1, has_above)
                    outs += [(always, 0, mine, 1)]
                    outs += [(onward, way, origin, half) for origin, half in ((mine, 1), (mine, 0), (other, 0))]
                for cond, way, origin, half in outs:
                    copy = piece_copy(way, origin, half, beside, False)
                    pl.when(jnp.logical_and(there, cond))(copy.wait_send)
    else:
        copies = []
        for k in range(1, offsets):
            copies.append(pltpu.make_async_remote_copy(
                src_ref=g_ref, dst_ref=gall_ref.at[row], send_sem=send_sem.at[0, k, 0], recv_sem=recv_sem.at[k, 0],
                device_id=(lax.rem(row + k, n_row), rep), device_id_type=MESH))
        for copy in copies:
            copy.start()
        start_rest()
        for load in loads:
            load.wait()
        for copy in feat_copies + copies:
            copy.wait()


def gather(grad_out, features, weight, tile_vals, n_row, n_rep):
    offsets, slots, tile = tile_vals.shape[2:5]
    rows_dev, hidden = grad_out.shape
    chain = n_row == offsets and n_row % 2 == 0 and n_row >= 4 and rows_dev == 2 * tile
    vmem = pl.BlockSpec(memory_space=pltpu.VMEM)
    dma = pltpu.SemaphoreType.DMA
    return pl.pallas_call(
        functools.partial(gather_kernel, n_row, n_rep, offsets, chain),
        out_shape=(
            jax.ShapeDtypeStruct((n_row + 1, rows_dev // tile, tile, hidden), grad_out.dtype),
            jax.ShapeDtypeStruct((n_rep,) + features.shape, features.dtype),
            jax.ShapeDtypeStruct(weight.shape, weight.dtype),
            jax.ShapeDtypeStruct(tile_vals.shape[2:], tile_vals.dtype),
        ),
        in_specs=[pl.BlockSpec(memory_space=pltpu.HBM)] * 4,
        out_specs=(vmem,) * 4,
        scratch_shapes=[
            dma((3, n_row, 2)),
            dma((n_row, 2)),
            dma((n_rep,)),
            dma((n_rep,)),
            dma((3,)),
            dma((offsets,)),
        ],
        compiler_params=pltpu.CompilerParams(collective_id=0, has_side_effects=True, vmem_limit_bytes=24 * 2**20),
        name="gather_sources",
    )(*map(in_hbm, (grad_out.reshape(rows_dev // tile, tile, hidden), features, weight, tile_vals)))


def dot_first(left, right):
    return lax.dot_general(left, right, (((0,), (0,)), ((), ())), preferred_element_type=jnp.float32)


def split(value):
    high = value.astype(jnp.bfloat16)
    low = (value - high.astype(jnp.float32)).astype(jnp.bfloat16)
    return high, low


def tiles_kernel(offsets, tile, col_tiles, rows_in, cols_in, counts_in, vals, blocks, fall_ref, weight_ref, ig_ref, wg_ref, totals, rows_ref, cols_ref, counts_ref, sem):
    loads = [
        pltpu.make_async_copy(rows_in, rows_ref, sem.at[0]),
        pltpu.make_async_copy(cols_in, cols_ref, sem.at[1]),
        pltpu.make_async_copy(counts_in, counts_ref, sem.at[2]),
    ]
    for load in loads:
        load.start()
    totals[...] = jnp.zeros_like(totals)
    row, n_row = lax.axis_index("row"), lax.axis_size("row")
    for load in loads:
        load.wait()

    def one_offset(s, carry):
        count = counts_ref[0, 0, s]
        origin = lax.rem(row + n_row - s, n_row)

        def one_group(group, carry):
            parts = []
            for u in range(GROUP):
                k = group * GROUP + u
                chosen = blocks[jnp.where(k < count, origin, n_row), rows_ref[0, 0, s, k]]
                parts.append((cols_ref[0, 0, s, k], dot_first(vals[s, k], chosen)))
            for col, part in parts:
                totals[col] += part
            return carry

        return lax.fori_loop(0, (count + GROUP - 1) // GROUP, one_group, carry)

    lax.fori_loop(0, offsets, one_offset, 0)
    weight = weight_ref[...]
    feats, hidden = weight.shape

    def one_col(col, wg):
        high, low = split(totals[col])
        dims = (((1,), (1,)), ((), ()))
        ig_ref[col] = (
            lax.dot_general(high, weight, dims, preferred_element_type=jnp.float32)
            + lax.dot_general(low, weight, dims, preferred_element_type=jnp.float32))
        return wg + dot_first(fall_ref[col], high) + dot_first(fall_ref[col], low)

    wg = jnp.zeros((feats, hidden), jnp.float32)
    if col_tiles <= 8:
        for col in range(col_tiles):
            wg = one_col(col, wg)
    else:
        wg = lax.fori_loop(0, col_tiles, one_col, wg)
    for chunk in range(wg_ref.shape[0]):
        i, j = chunk // (hidden // 128), chunk % (hidden // 128)
        wg_ref[chunk] = wg[8 * i:8 * i + 8, 128 * j:128 * j + 128]


def tile_products(tile_rows, tile_cols, tile_counts, vals, gall, fall, weight):
    offsets, slots, tile = vals.shape[:3]
    row_tiles, hidden = gall.shape[1], gall.shape[3]
    n_rep, _, feats = fall.shape
    col_tiles = n_rep * row_tiles
    vmem = pl.BlockSpec(memory_space=pltpu.VMEM)
    hbm = pl.BlockSpec(memory_space=pltpu.HBM)
    return pl.pallas_call(
        functools.partial(tiles_kernel, offsets, tile, col_tiles),
        out_shape=(
            jax.ShapeDtypeStruct((col_tiles, tile, feats), jnp.float32),
            jax.ShapeDtypeStruct((feats * hidden // 1024, 8, 128), jnp.float32),
        ),
        in_specs=[hbm, hbm, hbm, vmem, vmem, vmem, vmem],
        out_specs=(vmem, vmem),
        scratch_shapes=[
            pltpu.VMEM((col_tiles, tile, hidden), jnp.float32),
            pltpu.SMEM(tile_rows.shape, jnp.int32),
            pltpu.SMEM(tile_cols.shape, jnp.int32),
            pltpu.SMEM(tile_counts.shape, jnp.int32),
            pltpu.SemaphoreType.DMA((3,)),
        ],
        compiler_params=pltpu.CompilerParams(vmem_limit_bytes=32 * 2**20),
        name="tile_products",
    )(in_hbm(tile_rows), in_hbm(tile_cols), in_hbm(tile_counts), vals, gall, fall.reshape(col_tiles, tile, feats), weight)


def reduce_kernel(n_row, n_rep, ig_ref, wg_ref, out_ref, wout_ref, pair_buf, mid_buf, ig_buf, wg_buf, row_buf, sum_buf, full_buf, pair_send, pair_recv, ig_send, ig_recv, wg_send, wg_recv, row_send, row_recv, full_send, full_recv):
    row, rep = lax.axis_index("row"), lax.axis_index("rep")
    pairs = n_rep // 2
    pair, core = rep // 2, rep % 2
    chunks = wg_ref.shape[1]
    scatter = chunks % n_row == 0
    share = chunks // n_row if scatter else chunks
    barrier = pltpu.get_barrier_semaphore()
    peers = [(i, j) for i in range(n_row) for j in range(n_rep) if (i or j) and (scatter or not (i and j))]
    for i, j in peers:
        pl.semaphore_signal(
            barrier, inc=1, device_id=(lax.rem(row + i, n_row), lax.rem(rep + j, n_rep)), device_id_type=MESH)
    pl.semaphore_wait(barrier, len(peers))

    started = []

    def copy_to(src, dst, send, recv, target):
        copy = pltpu.make_async_remote_copy(
            src_ref=src, dst_ref=dst, send_sem=send, recv_sem=recv, device_id=target, device_id_type=MESH)
        copy.start()
        started.append(copy)
        return copy

    wg_copies, pair_copies, ig_copies, row_copies, full_copies = [], [], [], [], []
    for k in range(1, n_rep):
        other = lax.rem(rep + k, n_rep)
        wg_copies.append(copy_to(wg_ref.at[other], wg_buf.at[rep], wg_send.at[k], wg_recv.at[k], (row, other)))
    for k in range(1, pairs + 1):
        block = lax.rem(pair + k, pairs)
        pair_copies.append(copy_to(
            ig_ref.at[block * 2 + 1 - core], pair_buf.at[block], pair_send.at[k - 1], pair_recv.at[k - 1],
            (row, rep + 1 - 2 * core)))
    for k in range(1, pairs):
        block = lax.rem(pair + k, pairs)
        pair_copies[k - 1].wait_recv()
        mid_buf[block] = ig_ref[block * 2 + core] + pair_buf[block]
        ig_copies.append(copy_to(
            mid_buf.at[block], ig_buf.at[pair], ig_send.at[k], ig_recv.at[k], (row, block * 2 + core)))
    wg_buf[rep] = wg_ref[rep]
    for copy in wg_copies:
        copy.wait_recv()
    total = wg_buf[0]
    for k in range(1, n_rep):
        total = total + wg_buf[k]
    sum_buf[...] = total.reshape(sum_buf.shape)
    for k in range(1, n_row):
        other = lax.rem(row + k, n_row)
        source = sum_buf.at[other] if scatter else sum_buf.at[0]
        row_copies.append(copy_to(source, row_buf.at[row], row_send.at[k], row_recv.at[k], (other, rep)))
    row_buf[row] = sum_buf[row] if scatter else sum_buf[0]
    for copy in row_copies:
        copy.wait_recv()
    total = row_buf[0]
    for k in range(1, n_row):
        total = total + row_buf[k]
    if scatter:
        full_buf[rep, row] = total
        for i, j in peers:
            full_copies.append(copy_to(
                full_buf.at[rep, row], full_buf.at[rep, row], full_send.at[i, j], full_recv.at[i, j],
                (lax.rem(row + i, n_row), lax.rem(rep + j, n_rep))))
    else:
        full_buf[rep, 0] = total
        for k in range(1, n_rep):
            other = lax.rem(rep + k, n_rep)
            full_copies.append(copy_to(
                full_buf.at[rep], full_buf.at[rep], full_send.at[0, k], full_recv.at[0, k], (row, other)))
    pair_copies[pairs - 1].wait_recv()
    total = ig_ref[rep] + pair_buf[pair]
    for k in range(1, pairs):
        ig_copies[k - 1].wait_recv()
        total = total + ig_buf[lax.rem(pair - k + pairs, pairs)]
    out_ref[...] = total.astype(out_ref.dtype)
    for copy in full_copies:
        copy.wait_recv()
    across = wout_ref.shape[1] // 128
    full = full_buf[...].reshape((n_rep * chunks, 8, 128))
    for chunk in range(n_rep * chunks):
        i, j = chunk // across, chunk % across
        wout_ref[8 * i:8 * i + 8, 128 * j:128 * j + 128] = full[chunk]
    for copy in started:
        copy.wait_send()


def reduce(ig_part, wg_part, feats, hidden, n_row, n_rep):
    chunks = wg_part.shape[0] // n_rep
    scatter = chunks % n_row == 0
    owners = n_row if scatter else 1
    share = chunks // owners
    rows_dev = ig_part.shape[0] * ig_part.shape[1] // n_rep
    width = ig_part.shape[2]
    pairs = n_rep // 2
    vmem = pl.BlockSpec(memory_space=pltpu.VMEM)
    dma = pltpu.SemaphoreType.DMA
    return pl.pallas_call(
        functools.partial(reduce_kernel, n_row, n_rep),
        out_shape=(
            jax.ShapeDtypeStruct((rows_dev, width), jnp.bfloat16),
            jax.ShapeDtypeStruct((feats, hidden), jnp.float32),
        ),
        in_specs=[vmem, vmem],
        out_specs=(vmem, vmem),
        scratch_shapes=[
            pltpu.VMEM((pairs, rows_dev, width), jnp.float32),
            pltpu.VMEM((pairs, rows_dev, width), jnp.float32),
            pltpu.VMEM((pairs, rows_dev, width), jnp.float32),
            pltpu.VMEM((n_rep, chunks, 8, 128), jnp.float32),
            pltpu.VMEM((n_row, share, 8, 128), jnp.float32),
            pltpu.VMEM((owners, share, 8, 128), jnp.float32),
            pltpu.VMEM((n_rep, owners, share, 8, 128), jnp.float32),
            dma((pairs,)), dma((pairs,)), dma((pairs,)), dma((pairs,)),
            dma((n_rep,)), dma((n_rep,)), dma((n_row,)), dma((n_row,)),
            dma((n_row, n_rep)), dma((n_row, n_rep)),
        ],
        compiler_params=pltpu.CompilerParams(collective_id=1, has_side_effects=True, vmem_limit_bytes=32 * 2**20),
        name="reduce_grads",
    )(ig_part.reshape(n_rep, rows_dev, width), wg_part.reshape(n_rep, chunks, 8, 128))


def on_device(features, grad_out, weight, tile_vals, tile_rows, tile_cols, tile_counts):
    n_row, n_rep = lax.axis_size("row"), lax.axis_size("rep")
    gall, fall, weight_near, vals = gather(grad_out, features, weight, tile_vals, n_row, n_rep)
    ig_part, wg_part = tile_products(tile_rows, tile_cols, tile_counts, vals, gall, fall, weight_near)
    return reduce(ig_part, wg_part, weight.shape[0], weight.shape[1], n_row, n_rep)


def solution(mesh):
    placed = (
        P(("row", "rep"), None),
        P(("row", "rep"), None),
        P(),
        P("row", "rep", None, None, None, None),
        P("row", "rep", None, None),
        P("row", "rep", None, None),
        P("row", "rep", None),
    )
    return jax.shard_map(
        on_device,
        mesh=mesh,
        in_specs=placed,
        out_specs=(P(("row", "rep"), None), P()),
        check_vma=False,
    )
```

```python
import functools

import jax
import jax.numpy as jnp
from jax import lax
from jax.experimental import pallas as pl
from jax.experimental.pallas import tpu as pltpu
from jax.sharding import PartitionSpec as P

MESH = pl.DeviceIdType.MESH
GROUP = 40


def in_hbm(value):
    return pltpu.with_memory_space_constraint(value, pltpu.HBM)


def gather_kernel(n_row, n_rep, offsets, chain, g_ref, f_ref, weight_in, vals_in, gall_ref, fall_ref, weight_ref, vals_ref, send_sem, recv_sem, fsend_sem, frecv_sem, local_sem, vals_sem):
    row, rep = lax.axis_index("row"), lax.axis_index("rep")
    barrier = pltpu.get_barrier_semaphore()
    loads = [
        pltpu.make_async_copy(g_ref, gall_ref.at[row], local_sem.at[0]),
        pltpu.make_async_copy(f_ref, fall_ref.at[rep], local_sem.at[1]),
        pltpu.make_async_copy(weight_in, weight_ref, local_sem.at[2]),
    ]
    for s in range(offsets):
        loads.append(pltpu.make_async_copy(vals_in.at[0, 0, s], vals_ref.at[s], vals_sem.at[s]))

    for load in loads:
        load.start()

    def piece_copy(way, origin, half, target, own):
        return pltpu.make_async_remote_copy(
            src_ref=g_ref.at[half] if own else gall_ref.at[origin, half],
            dst_ref=gall_ref.at[origin, half],
            send_sem=send_sem.at[way, origin, half],
            recv_sem=recv_sem.at[origin, half],
            device_id=(target, rep), device_id_type=MESH)

    for k in range(1, n_rep):
        pl.semaphore_signal(barrier, inc=1, device_id=(row, lax.rem(rep + k, n_rep)), device_id_type=MESH)
    if chain:
        z, y = row // 2, row % 2
        length = n_row // 2
        beside, above, below = row + 1 - 2 * y, row + 2, row - 2
        has_above, has_below = z < length - 1, z > 0
        pl.semaphore_signal(barrier, inc=1, device_id=(beside, rep), device_id_type=MESH)

        @pl.when(has_above)
        def _():
            pl.semaphore_signal(barrier, inc=1, device_id=(above, rep), device_id_type=MESH)

        @pl.when(has_below)
        def _():
            pl.semaphore_signal(barrier, inc=1, device_id=(below, rep), device_id_type=MESH)

        pl.semaphore_wait(barrier, n_rep + has_above.astype(jnp.int32) + has_below.astype(jnp.int32))
    else:
        shifts = sorted({k % n_row for k in range(1, offsets)} | {-k % n_row for k in range(1, offsets)})
        for k in shifts:
            pl.semaphore_signal(barrier, inc=1, device_id=(lax.rem(row + k, n_row), rep), device_id_type=MESH)
        pl.semaphore_wait(barrier, len(shifts) + n_rep - 1)

    feat_copies = []
    for k in range(1, n_rep):
        feat_copies.append(pltpu.make_async_remote_copy(
            src_ref=f_ref, dst_ref=fall_ref.at[rep], send_sem=fsend_sem.at[k], recv_sem=frecv_sem.at[k],
            device_id=(row, lax.rem(rep + k, n_rep)), device_id_type=MESH))

    def start_rest():
        for copy in feat_copies:
            copy.start()
        gall_ref[n_row] = jnp.zeros(gall_ref.shape[1:], gall_ref.dtype)

    if chain:
        def send(cond, way, origin, half, target, own=False):
            pl.when(cond)(piece_copy(way, origin, half, target, own).start)

        always = row >= 0
        send(always, 0, row, 0, beside, True)
        send(has_above, 1, row, 1, above, True)
        send(has_below, 2, row, 1, below, True)
        send(has_above, 1, row, 0, above, True)
        send(has_below, 2, row, 0, below, True)
        send(always, 0, row, 1, beside, True)
        start_rest()
        piece_copy(0, beside, 0, beside, False).wait_recv()
        send(has_above, 1, beside, 0, above)
        send(has_below, 2, beside, 0, below)
        for dist in range(1, length):
            for item in range(3):
                for down in (False, True):
                    far = z + dist if down else z - dist
                    there = far < length if down else far >= 0
                    origin = far * 2 + (1 - y if item == 2 else y)
                    half = 1 if item == 0 else 0
                    way, onward, target = (2, has_below, below) if down else (1, has_above, above)

                    @pl.when(there)
                    def _():
                        piece_copy(0, origin, half, beside, False).wait_recv()
                        send(onward, way, origin, half, target)
                        if item == 0:
                            send(always, 0, origin, half, beside)

        piece_copy(0, beside, 1, beside, False).wait_recv()
        for dist in range(1, length):
            for down in (False, True):
                far = z + dist if down else z - dist
                there = far < length if down else far >= 0
                other = far * 2 + 1 - y

                @pl.when(there)
                def _():
                    piece_copy(0, other, 1, beside, False).wait_recv()

        for load in loads:
            load.wait()
        for copy in feat_copies:
            copy.wait()
        for dist in range(length):
            for down in (False, True) if dist else (False,):
                far = z + dist if down else z - dist
                there = far < length if down else far >= 0
                mine, other = far * 2 + y, far * 2 + 1 - y
                outs = []
                if dist == 0:
                    outs += [(always, 0, mine, 0), (always, 0, mine, 1)]
                    for origin, half in ((mine, 0), (mine, 1), (other, 0)):
                        outs += [(has_above, 1, origin, half), (has_below, 2, origin, half)]
                else:
                    way, onward = (2, has_below) if down else (1, has_above)
                    outs += [(always, 0, mine, 1)]
                    outs += [(onward, way, origin, half) for origin, half in ((mine, 1), (mine, 0), (other, 0))]
                for cond, way, origin, half in outs:
                    copy = piece_copy(way, origin, half, beside, False)
                    pl.when(jnp.logical_and(there, cond))(copy.wait_send)
    else:
        copies = []
        for k in range(1, offsets):
            copies.append(pltpu.make_async_remote_copy(
                src_ref=g_ref, dst_ref=gall_ref.at[row], send_sem=send_sem.at[0, k, 0], recv_sem=recv_sem.at[k, 0],
                device_id=(lax.rem(row + k, n_row), rep), device_id_type=MESH))
        for copy in copies:
            copy.start()
        start_rest()
        for load in loads:
            load.wait()
        for copy in feat_copies + copies:
            copy.wait()


def gather(grad_out, features, weight, tile_vals, n_row, n_rep):
    offsets, slots, tile = tile_vals.shape[2:5]
    rows_dev, hidden = grad_out.shape
    chain = n_row == offsets and n_row % 2 == 0 and n_row >= 4 and rows_dev == 2 * tile
    vmem = pl.BlockSpec(memory_space=pltpu.VMEM)
    dma = pltpu.SemaphoreType.DMA
    return pl.pallas_call(
        functools.partial(gather_kernel, n_row, n_rep, offsets, chain),
        out_shape=(
            jax.ShapeDtypeStruct((n_row + 1, rows_dev // tile, tile, hidden), grad_out.dtype),
            jax.ShapeDtypeStruct((n_rep,) + features.shape, features.dtype),
            jax.ShapeDtypeStruct(weight.shape, weight.dtype),
            jax.ShapeDtypeStruct(tile_vals.shape[2:], tile_vals.dtype),
        ),
        in_specs=[pl.BlockSpec(memory_space=pltpu.HBM)] * 4,
        out_specs=(vmem,) * 4,
        scratch_shapes=[
            dma((3, n_row, 2)),
            dma((n_row, 2)),
            dma((n_rep,)),
            dma((n_rep,)),
            dma((3,)),
            dma((offsets,)),
        ],
        compiler_params=pltpu.CompilerParams(collective_id=0, has_side_effects=True, vmem_limit_bytes=24 * 2**20),
        name="gather_sources",
    )(*map(in_hbm, (grad_out.reshape(rows_dev // tile, tile, hidden), features, weight, tile_vals)))


def dot_first(left, right):
    return lax.dot_general(left, right, (((0,), (0,)), ((), ())), preferred_element_type=jnp.float32)


def split(value):
    high = value.astype(jnp.bfloat16)
    low = (value - high.astype(jnp.float32)).astype(jnp.bfloat16)
    return high, low


def tiles_kernel(offsets, tile, col_tiles, rows_in, cols_in, counts_in, vals, blocks, fall_ref, weight_ref, ig_ref, wg_ref, totals, rows_ref, cols_ref, counts_ref, sem):
    loads = [
        pltpu.make_async_copy(rows_in, rows_ref, sem.at[0]),
        pltpu.make_async_copy(cols_in, cols_ref, sem.at[1]),
        pltpu.make_async_copy(counts_in, counts_ref, sem.at[2]),
    ]
    for load in loads:
        load.start()
    totals[...] = jnp.zeros_like(totals)
    row, n_row = lax.axis_index("row"), lax.axis_size("row")
    for load in loads:
        load.wait()

    def one_offset(s, carry):
        count = counts_ref[0, 0, s]
        origin = lax.rem(row + n_row - s, n_row)

        def one_group(group, carry):
            parts = []
            for u in range(GROUP):
                k = group * GROUP + u
                chosen = blocks[jnp.where(k < count, origin, n_row), rows_ref[0, 0, s, k]]
                parts.append((cols_ref[0, 0, s, k], dot_first(vals[s, k], chosen)))
            for col, part in parts:
                totals[col] += part
            return carry

        return lax.fori_loop(0, (count + GROUP - 1) // GROUP, one_group, carry)

    lax.fori_loop(0, offsets, one_offset, 0)
    weight = weight_ref[...]
    feats, hidden = weight.shape

    def one_col(col, wg):
        high, low = split(totals[col])
        dims = (((1,), (1,)), ((), ()))
        ig_ref[col] = (
            lax.dot_general(high, weight, dims, preferred_element_type=jnp.float32)
            + lax.dot_general(low, weight, dims, preferred_element_type=jnp.float32))
        return wg + dot_first(fall_ref[col], high) + dot_first(fall_ref[col], low)

    wg = jnp.zeros((feats, hidden), jnp.float32)
    if col_tiles <= 8:
        for col in range(col_tiles):
            wg = one_col(col, wg)
    else:
        wg = lax.fori_loop(0, col_tiles, one_col, wg)
    for chunk in range(wg_ref.shape[0]):
        i, j = chunk // (hidden // 128), chunk % (hidden // 128)
        wg_ref[chunk] = wg[8 * i:8 * i + 8, 128 * j:128 * j + 128]


def tile_products(tile_rows, tile_cols, tile_counts, vals, gall, fall, weight):
    offsets, slots, tile = vals.shape[:3]
    row_tiles, hidden = gall.shape[1], gall.shape[3]
    n_rep, _, feats = fall.shape
    col_tiles = n_rep * row_tiles
    vmem = pl.BlockSpec(memory_space=pltpu.VMEM)
    hbm = pl.BlockSpec(memory_space=pltpu.HBM)
    return pl.pallas_call(
        functools.partial(tiles_kernel, offsets, tile, col_tiles),
        out_shape=(
            jax.ShapeDtypeStruct((col_tiles, tile, feats), jnp.float32),
            jax.ShapeDtypeStruct((feats * hidden // 1024, 8, 128), jnp.float32),
        ),
        in_specs=[hbm, hbm, hbm, vmem, vmem, vmem, vmem],
        out_specs=(vmem, vmem),
        scratch_shapes=[
            pltpu.VMEM((col_tiles, tile, hidden), jnp.float32),
            pltpu.SMEM(tile_rows.shape, jnp.int32),
            pltpu.SMEM(tile_cols.shape, jnp.int32),
            pltpu.SMEM(tile_counts.shape, jnp.int32),
            pltpu.SemaphoreType.DMA((3,)),
        ],
        compiler_params=pltpu.CompilerParams(vmem_limit_bytes=32 * 2**20),
        name="tile_products",
    )(in_hbm(tile_rows), in_hbm(tile_cols), in_hbm(tile_counts), vals, gall, fall.reshape(col_tiles, tile, feats), weight)


def reduce_kernel(n_row, n_rep, ig_ref, wg_ref, out_ref, wout_ref, pair_buf, mid_buf, ig_buf, wg_buf, row_buf, sum_buf, full_buf, pair_send, pair_recv, ig_send, ig_recv, wg_send, wg_recv, row_send, row_recv, full_send, full_recv, all_buf, all_send, all_recv):
    row, rep = lax.axis_index("row"), lax.axis_index("rep")
    pairs = n_rep // 2
    pair, core = rep // 2, rep % 2
    chunks = wg_ref.shape[1]
    scatter = chunks % n_row == 0
    share = chunks // n_row if scatter else chunks
    barrier = pltpu.get_barrier_semaphore()
    peers = [(i, j) for i in range(n_row) for j in range(n_rep) if (i or j) and (scatter or not (i and j))]
    for i, j in peers:
        pl.semaphore_signal(
            barrier, inc=1, device_id=(lax.rem(row + i, n_row), lax.rem(rep + j, n_rep)), device_id_type=MESH)
    pl.semaphore_wait(barrier, len(peers))

    started = []

    def copy_to(src, dst, send, recv, target):
        copy = pltpu.make_async_remote_copy(
            src_ref=src, dst_ref=dst, send_sem=send, recv_sem=recv, device_id=target, device_id_type=MESH)
        copy.start()
        started.append(copy)
        return copy

    wg_copies, pair_copies, ig_copies, row_copies, full_copies = [], [], [], [], []
    for i, j in peers if scatter else ():
        to_row, to_rep = lax.rem(row + i, n_row), lax.rem(rep + j, n_rep)
        row_copies.append(copy_to(
            wg_ref.at[to_rep, pl.ds(to_row * share, share)], all_buf.at[row, rep], all_send.at[i, j], all_recv.at[i, j],
            (to_row, to_rep)))
    for k in range(1, 1 if scatter else n_rep):
        other = lax.rem(rep + k, n_rep)
        wg_copies.append(copy_to(wg_ref.at[other], wg_buf.at[rep], wg_send.at[k], wg_recv.at[k], (row, other)))
    for k in range(1, pairs + 1):
        block = lax.rem(pair + k, pairs)
        pair_copies.append(copy_to(
            ig_ref.at[block * 2 + 1 - core], pair_buf.at[block], pair_send.at[k - 1], pair_recv.at[k - 1],
            (row, rep + 1 - 2 * core)))
    for k in range(1, pairs):
        block = lax.rem(pair + k, pairs)
        pair_copies[k - 1].wait_recv()
        mid_buf[block] = ig_ref[block * 2 + core] + pair_buf[block]
        ig_copies.append(copy_to(
            mid_buf.at[block], ig_buf.at[pair], ig_send.at[k], ig_recv.at[k], (row, block * 2 + core)))
    if scatter:
        all_buf[row, rep] = wg_ref[rep, pl.ds(row * share, share)]
        for copy in row_copies:
            copy.wait_recv()
        total = jnp.sum(all_buf[...], axis=(0, 1))
    else:
        wg_buf[rep] = wg_ref[rep]
        for copy in wg_copies:
            copy.wait_recv()
        total = wg_buf[0]
        for k in range(1, n_rep):
            total = total + wg_buf[k]
        sum_buf[...] = total.reshape(sum_buf.shape)
        for k in range(1, n_row):
            other = lax.rem(row + k, n_row)
            source = sum_buf.at[0]
            row_copies.append(copy_to(source, row_buf.at[row], row_send.at[k], row_recv.at[k], (other, rep)))
        row_buf[row] = sum_buf[0]
        for copy in row_copies:
            copy.wait_recv()
        total = row_buf[0]
        for k in range(1, n_row):
            total = total + row_buf[k]
    if scatter:
        full_buf[rep, row] = total
        for i, j in peers:
            full_copies.append(copy_to(
                full_buf.at[rep, row], full_buf.at[rep, row], full_send.at[i, j], full_recv.at[i, j],
                (lax.rem(row + i, n_row), lax.rem(rep + j, n_rep))))
    else:
        full_buf[rep, 0] = total
        for k in range(1, n_rep):
            other = lax.rem(rep + k, n_rep)
            full_copies.append(copy_to(
                full_buf.at[rep], full_buf.at[rep], full_send.at[0, k], full_recv.at[0, k], (row, other)))
    pair_copies[pairs - 1].wait_recv()
    total = ig_ref[rep] + pair_buf[pair]
    for k in range(1, pairs):
        ig_copies[k - 1].wait_recv()
        total = total + ig_buf[lax.rem(pair - k + pairs, pairs)]
    out_ref[...] = total.astype(out_ref.dtype)
    for copy in full_copies:
        copy.wait_recv()
    across = wout_ref.shape[1] // 128
    full = full_buf[...].reshape((n_rep * chunks, 8, 128))
    for chunk in range(n_rep * chunks):
        i, j = chunk // across, chunk % across
        wout_ref[8 * i:8 * i + 8, 128 * j:128 * j + 128] = full[chunk]
    for copy in started:
        copy.wait_send()


def reduce(ig_part, wg_part, feats, hidden, n_row, n_rep):
    chunks = wg_part.shape[0] // n_rep
    scatter = chunks % n_row == 0
    owners = n_row if scatter else 1
    share = chunks // owners
    rows_dev = ig_part.shape[0] * ig_part.shape[1] // n_rep
    width = ig_part.shape[2]
    pairs = n_rep // 2
    vmem = pl.BlockSpec(memory_space=pltpu.VMEM)
    dma = pltpu.SemaphoreType.DMA
    return pl.pallas_call(
        functools.partial(reduce_kernel, n_row, n_rep),
        out_shape=(
            jax.ShapeDtypeStruct((rows_dev, width), jnp.bfloat16),
            jax.ShapeDtypeStruct((feats, hidden), jnp.float32),
        ),
        in_specs=[vmem, vmem],
        out_specs=(vmem, vmem),
        scratch_shapes=[
            pltpu.VMEM((pairs, rows_dev, width), jnp.float32),
            pltpu.VMEM((pairs, rows_dev, width), jnp.float32),
            pltpu.VMEM((pairs, rows_dev, width), jnp.float32),
            pltpu.VMEM((n_rep, chunks, 8, 128), jnp.float32),
            pltpu.VMEM((n_row, share, 8, 128), jnp.float32),
            pltpu.VMEM((owners, share, 8, 128), jnp.float32),
            pltpu.VMEM((n_rep, owners, share, 8, 128), jnp.float32),
            dma((pairs,)), dma((pairs,)), dma((pairs,)), dma((pairs,)),
            dma((n_rep,)), dma((n_rep,)), dma((n_row,)), dma((n_row,)),
            dma((n_row, n_rep)), dma((n_row, n_rep)),
            pltpu.VMEM((n_row, n_rep, share, 8, 128), jnp.float32),
            dma((n_row, n_rep)), dma((n_row, n_rep)),
        ],
        compiler_params=pltpu.CompilerParams(collective_id=1, has_side_effects=True, vmem_limit_bytes=32 * 2**20),
        name="reduce_grads",
    )(ig_part.reshape(n_rep, rows_dev, width), wg_part.reshape(n_rep, chunks, 8, 128))


def on_device(features, grad_out, weight, tile_vals, tile_rows, tile_cols, tile_counts):
    n_row, n_rep = lax.axis_size("row"), lax.axis_size("rep")
    gall, fall, weight_near, vals = gather(grad_out, features, weight, tile_vals, n_row, n_rep)
    ig_part, wg_part = tile_products(tile_rows, tile_cols, tile_counts, vals, gall, fall, weight_near)
    return reduce(ig_part, wg_part, weight.shape[0], weight.shape[1], n_row, n_rep)


def solution(mesh):
    placed = (
        P(("row", "rep"), None),
        P(("row", "rep"), None),
        P(),
        P("row", "rep", None, None, None, None),
        P("row", "rep", None, None),
        P("row", "rep", None, None),
        P("row", "rep", None),
    )
    return jax.shard_map(
        on_device,
        mesh=mesh,
        in_specs=placed,
        out_specs=(P(("row", "rep"), None), P()),
        check_vma=False,
    )
```
